32 devices in a mesh: fsdp: 8 (over y, x, core), win: 4 (over z).
Axes of the slice: x: 2, y: 2, z: 4, core: 2. Of those that a mesh axis runs over, the one named last changes fastest.
Arguments:
- tokens: bfloat16 [16384, 2048], P(('fsdp', 'win')), may hold values from -16 to 16
- block_map: int32 [8, 4], P('fsdp'), may hold values from 0 to 3, each once within a row
- shift: int32 [8], P('fsdp'), may hold values from 1 to 2047
- ln_gain: float32 [2048], replicated, may hold values from 0.5 to 1.5
- w_query: bfloat16 [2048, 1024], P('fsdp'), may hold values from -1 to 1
- w_key: bfloat16 [2048, 1024], P('fsdp'), may hold values from -1 to 1
- w_value: bfloat16 [2048, 1024], P('fsdp'), may hold values from -0.125 to 0.125
- w_out: bfloat16 [1024, 2048], P('fsdp'), may hold values from -0.1875 to 0.1875
- logit_scale: float32 [16], replicated, may hold values from 1 to 300
Outputs:
- mixed: bfloat16 [16384, 2048], P(('fsdp', 'win'))
The draws below stay inside these ranges and needn't reach their ends.
All inputs are finite; a program needn't handle non-finite values.
Results may differ from the reference program's by a relative error of at most 0.008.
Values may be sent and summed in bfloat16 or wider, within the bound.
A program may use at most 128 MiB of HBM per device.

```python
import math
import jax
import jax.numpy as jnp
from jax import lax

D = 2048
HEADS = 16
HEAD = 64
TOK_DEV = 512
HD = 1024
WIN = 2048
WINDOWS = 8
TOKENS = 16384
N_WIN = 4


def cluster_index(key):
    member_of = jax.random.randint(jax.random.fold_in(key, 6), (TOKENS,), 0, 8)
    window_of = jnp.arange(TOKENS, dtype=jnp.int32) // WIN
    return window_of * 8 + member_of


def draw_tokens(key, part):
    picked_rows = cluster_index(key)
    protos = jax.random.normal(jax.random.fold_in(key, 5), (WINDOWS * 8, D), jnp.float32)
    jitter = jax.random.normal(jax.random.fold_in(key, 8), (TOKENS, D), jnp.float32)
    base = jnp.take(protos, picked_rows, axis=0) + 0.5 * jitter
    return jnp.clip(base, -6.0, 6.0).astype(jnp.bfloat16)


def query_key_pair(key):
    first = jnp.clip(jax.random.normal(jax.random.fold_in(key, 11), (D, HD), jnp.float32), -5.0, 5.0)
    second = jnp.clip(jax.random.normal(jax.random.fold_in(key, 12), (D, HD), jnp.float32), -5.0, 5.0)
    second = jnp.clip(0.8 * first + 0.6 * second, -5.0, 5.0)
    factor = 1.0 / math.sqrt(D)
    return (jnp.clip(first * factor, -1.0, 1.0), jnp.clip(second * factor, -1.0, 1.0))


def draw_w_query(key, part):
    return query_key_pair(key)[0].astype(jnp.bfloat16)


def draw_w_key(key, part):
    return query_key_pair(key)[1].astype(jnp.bfloat16)


def touch_ends(values, stream_key, low, top_value):
    extent = values.shape
    spot = [jax.random.randint(jax.random.fold_in(stream_key, axis), (), 0, extent[axis]) for axis in range(len(extent))]
    values = values.at[tuple(spot)].set(low)
    longest = extent.index(max(extent))
    spot[longest] = (spot[longest] + 1) % extent[longest]
    return values.at[tuple(spot)].set(top_value)


def steps_of(rng, shape, shards, smallest, high):
    loudness, own = 1.0, jax.random.fold_in(rng, 6)
    for dim, parts in shards:
        draws = jnp.exp(jax.random.uniform(jax.random.fold_in(own, dim), (parts,), jnp.float32, smallest / len(shards), high / len(shards)))
        loudness = loudness * jnp.repeat(draws, shape[dim] // parts).reshape([-1 if axis == dim else 1 for axis in range(len(shape))])
    return loudness


def normal_values(key, extent, scale, reach, pieces=(), kind=jnp.bfloat16):
    drawn = jax.random.normal(key, extent, jnp.float32) * scale
    if len(pieces) > 0:
        drawn = steps_of(key, extent, pieces, -0.22, 0.18) * drawn
    return jnp.clip(drawn, min=-reach, max=reach).astype(kind)


def setup_inputs(seed: int = 0) -> dict:
    key_of = jax.random.split(jax.random.key(seed), 10)
    tokens = draw_tokens(jax.random.fold_in(key_of[9], 71), 0)
    block_map = jax.vmap(lambda own: jax.random.permutation(own, N_WIN))(jax.random.split(key_of[1], WINDOWS)).reshape((WINDOWS, N_WIN)).astype(jnp.int32)
    shift = touch_ends(jax.random.randint(key_of[2], (WINDOWS,), 1, WIN), jax.random.fold_in(key_of[2], 1), 1, WIN - 1).astype(jnp.int32)
    ln_gain = jnp.clip(1.0 + 0.1 * jax.random.normal(key_of[3], (D,), jnp.float32), 0.5, 1.5)
    w_query = draw_w_query(jax.random.fold_in(key_of[9], 71), 0)
    w_key = draw_w_key(jax.random.fold_in(key_of[9], 71), 0)
    w_value = normal_values(key_of[6], (D, HD), D ** -0.5, 0.125, ((0, 8),))
    w_out = normal_values(key_of[7], (HD, D), HD ** -0.5, 0.1875, ((0, 8),))
    logit_scale = jnp.clip(jnp.exp(jax.random.uniform(key_of[8], (HEADS,), jnp.float32, math.log(1.0), math.log(300.0))), 1.0, 300.0)
    return dict(tokens=tokens, block_map=block_map, shift=shift, ln_gain=ln_gain, w_query=w_query, w_key=w_key, w_value=w_value, w_out=w_out, logit_scale=logit_scale)


def layer_norm(resid, gain):
    center = lax.optimization_barrier(jnp.mean(resid, axis=-1, keepdims=True))
    centred = resid - center
    spread = lax.optimization_barrier(jnp.mean(centred * centred, axis=-1, keepdims=True))
    return (centred * lax.rsqrt(spread + 1e-05) * gain).astype(jnp.bfloat16)

def unit_heads(values, head_count):
    split = values.reshape(values.shape[0], head_count, -1)
    scale = lax.rsqrt(lax.optimization_barrier(jnp.sum(split * split, axis=-1, keepdims=True)) + 1e-06)
    return (split * scale).astype(jnp.bfloat16)

def reference(tokens, block_map, shift, ln_gain, w_query, w_key, w_value, w_out, logit_scale):

    def one_window(packed):
        window_x, order_row, offset = packed
        resid = window_x.astype(jnp.float32)
        normed = layer_norm(resid, ln_gain)
        query = jnp.dot(normed, w_query, preferred_element_type=jnp.float32)
        key_full = jnp.dot(normed, w_key, preferred_element_type=jnp.float32)
        value = jnp.dot(normed, w_value, preferred_element_type=jnp.float32).astype(jnp.bfloat16)
        q_unit = unit_heads(query, HEADS).astype(jnp.float32)
        k_unit = unit_heads(key_full, HEADS).astype(jnp.float32)
        value_heads = value.reshape(WIN, HEADS, HEAD).astype(jnp.float32)
        index = jnp.arange(WIN, dtype=jnp.int32)
        position = order_row[index // TOK_DEV] * TOK_DEV + index % TOK_DEV
        region = position >= offset
        allowed = region[:, None] == region[None, :]
        score = jnp.einsum('ihd,jhd->hij', q_unit, k_unit) * logit_scale[:, None, None]
        score = jnp.where(allowed[None], score, -1e+30)
        best = lax.optimization_barrier(jnp.max(score, axis=-1, keepdims=True))
        weight = jnp.where(allowed[None], jnp.exp(score - best), 0.0)
        probs = (weight / lax.optimization_barrier(jnp.sum(weight, axis=-1, keepdims=True))).astype(jnp.bfloat16)
        attended = jnp.einsum('hij,jhd->ihd', probs.astype(jnp.float32), value_heads)
        attended = attended.reshape(WIN, HD).astype(jnp.bfloat16)
        return (resid + jnp.dot(attended, w_out, preferred_element_type=jnp.float32)).astype(jnp.bfloat16)
    windows = tokens.reshape(WINDOWS, WIN, D)
    result = lax.map(one_window, (windows, block_map, shift))
    return result.reshape(TOKENS, D)
```

```python
import functools
import math

import jax
import jax.numpy as jnp
from jax import lax
from jax.experimental import pallas as pl
from jax.experimental.pallas import tpu as pltpu
from jax.sharding import PartitionSpec as P

MESH = pl.DeviceIdType.MESH
LANES = 128
FAR = 1024.0


def layer_kernel(
    sizes,
    tokens_ref, map_ref, shift_ref, gain_ref, wq_ref, wk_ref, wv_ref, wo_ref, scale_ref,
    out_ref,
    weights, w_out, normed, sent, held, keys_t, values_1, heads_out, attended,
    load_sem, p1_send, p1_recv, p2_send, p2_recv, p3_send, p3_recv,
    a2a_send, a2a_recv, back_send, back_recv,
):
    rows_a, rows_b, groups, head_size = sizes
    tok, width = tokens_ref.shape
    cols = weights.shape[-1]
    group_heads = cols // head_size
    pairs = cols // LANES
    me = lax.axis_index("fsdp")
    mine = lax.axis_index("win")
    at_a = me // (2 * rows_b)
    at_b = (me // 2) % rows_b
    at_c = me % 2

    def index_of(a, b, c):
        return (a * rows_b + b) * 2 + c

    a_peers = [index_of((at_a + i) % rows_a, at_b, at_c) for i in range(1, rows_a)]
    b_peers = [index_of(at_a, (at_b + i) % rows_b, at_c) for i in range(1, rows_b)]
    c_peer = index_of(at_a, at_b, 1 - at_c)

    barrier = pltpu.get_barrier_semaphore()
    greeted = 0
    for peer in a_peers + b_peers + [c_peer]:
        pl.semaphore_signal(barrier, inc=1, device_id=(peer, mine), device_id_type=MESH)
        greeted += 1
    for i in range(1, groups):
        pl.semaphore_signal(
            barrier, inc=1, device_id=(me, (mine + i) % groups), device_id_type=MESH
        )
        greeted += 1

    def loads(step):
        if step == groups:
            return [pltpu.make_async_copy(wo_ref, w_out.at[at_a, at_b, at_c], load_sem.at[step, 0])]
        group = (mine + 1 + step) % groups
        window = pl.ds(pl.multiple_of(group * cols, cols), cols)
        return [
            pltpu.make_async_copy(
                source.at[:, window], weights.at[step, m, at_a, at_b, at_c], load_sem.at[step, m]
            )
            for m, source in enumerate((wq_ref, wk_ref, wv_ref))
        ]

    for step in range(groups + 1):
        for copy in loads(step):
            copy.start()
    pl.semaphore_wait(barrier, greeted)

    def view(step, a, b, c, half):
        if step == groups:
            part = w_out.shape[-1] // 2
            return w_out.at[a, b, c, :, pl.ds(half * part, part)]
        part = cols // 2
        return weights.at[step, :, a, b, c, :, pl.ds(half * part, part)]

    def everything(count):
        return pl.ds(0, count)

    def push(ref, send, recv, peer):
        return pltpu.make_async_remote_copy(
            src_ref=ref, dst_ref=ref, send_sem=send, recv_sem=recv,
            device_id=(peer, mine), device_id_type=MESH,
        )

    def phase1(step):
        for half, peers in ((0, a_peers), (1, b_peers)):
            for peer in peers:
                push(
                    view(step, at_a, at_b, at_c, half),
                    p1_send.at[step, half], p1_recv.at[step, half], peer,
                ).start()

    def phase1_size(step, half):
        if half == 0:
            return view(step, pl.ds(0, rows_a - 1), at_b, at_c, 0)
        return view(step, at_a, pl.ds(0, rows_b - 1), at_c, 1)

    def phase2(step):
        for peer in b_peers:
            push(
                view(step, everything(rows_a), at_b, at_c, 0),
                p2_send.at[step, 0], p2_recv.at[step, 0], peer,
            ).start()
        for peer in a_peers:
            push(
                view(step, at_a, everything(rows_b), at_c, 1),
                p2_send.at[step, 1], p2_recv.at[step, 1], peer,
            ).start()

    def phase2_size(step, half):
        if half == 0:
            return view(step, everything(rows_a), pl.ds(0, rows_b - 1), at_c, 0)
        return view(step, pl.ds(0, rows_a - 1), everything(rows_b), at_c, 1)

    def phase3(step):
        if step == groups:
            ref = w_out.at[:, :, at_c]
        else:
            ref = weights.at[step, :, :, :, at_c]
        return push(ref, p3_send.at[step], p3_recv.at[step], c_peer)

    def drain(ref, sem):
        pltpu.make_async_copy(ref, ref, sem).wait()

    def wait1(step):
        for half in range(2):
            drain(phase1_size(step, half), p1_recv.at[step, half])

    def wait2(step):
        for half in range(2):
            drain(phase2_size(step, half), p2_recv.at[step, half])

    def own_loaded(step):
        for copy in loads(step):
            copy.wait()

    own_loaded(0)
    phase1(0)
    own_loaded(1)

    norm_tile = min(tok, 64)

    @pl.loop(0, tok // norm_tile)
    def _(i):
        part = pl.ds(pl.multiple_of(i * norm_tile, norm_tile), norm_tile)
        resid = tokens_ref[part, :].astype(jnp.float32)
        center = jnp.mean(resid, axis=-1, keepdims=True)
        centred = resid - center
        spread = jnp.mean(centred * centred, axis=-1, keepdims=True)
        normed[part, :] = (centred * lax.rsqrt(spread + 1e-05) * gain_ref[...]).astype(jnp.bfloat16)

    tile = min(tok, 256)
    row_head = lax.broadcasted_iota(jnp.int32, (cols, cols), 0) // head_size
    col_head = lax.broadcasted_iota(jnp.int32, (cols, cols), 1) // head_size
    same_head = (row_head == col_head).astype(jnp.float32).astype(jnp.bfloat16)

    def unit(x):
        square = x * x
        high = square.astype(jnp.bfloat16)
        low = (square - high.astype(jnp.float32)).astype(jnp.bfloat16)
        total = jnp.dot(high, same_head, preferred_element_type=jnp.float32)
        total += jnp.dot(low, same_head, preferred_element_type=jnp.float32)
        return (x * lax.rsqrt(total + 1e-06)).astype(jnp.bfloat16)

    def exchange(step):
        group = (mine + 1 + step) % groups
        return pltpu.make_async_remote_copy(
            src_ref=sent.at[step], dst_ref=held.at[mine],
            send_sem=a2a_send.at[step], recv_sem=a2a_recv.at[mine],
            device_id=(me, group), device_id_type=MESH,
        )

    def project(step):
        target = held.at[mine] if step == groups - 1 else sent.at[step]

        @pl.loop(0, tok // tile)
        def _(i):
            part = pl.ds(pl.multiple_of(i * tile, tile), tile)
            x = normed[part, :]
            for m in range(3):
                w = weights[step, m].reshape(width, cols)
                y = jnp.dot(x, w, preferred_element_type=jnp.float32)
                target[m, part, :] = unit(y) if m < 2 else y.astype(jnp.bfloat16)

        if step < groups - 1:
            exchange(step).start()

    for step in range(groups + 2):
        if step <= groups:
            wait1(step)
            phase2(step)
            if step + 1 <= groups:
                if step + 1 >= 2:
                    own_loaded(step + 1)
                phase1(step + 1)
        if 1 <= step <= groups:
            phase3(step - 1).wait_recv()
            project(step - 1)
        if step <= groups:
            wait2(step)
            phase3(step).start()

    def block_region(block, shape, axis, start):
        first = map_ref[0, block] * tok + start
        return (first + lax.broadcasted_iota(jnp.int32, shape, axis) >= shift_ref[0]).astype(jnp.float32)

    def prepare(block):
        where = pl.ds(pl.multiple_of(block * tok, tok), tok)
        region = block_region(block, (LANES, tok), 1, 0)
        row = lax.broadcasted_iota(jnp.int32, (LANES, tok), 0)
        feature = jnp.where(row == 0, region - 1.0, jnp.where(row == 1, -region, 0.0)) * FAR
        feature = feature.astype(jnp.bfloat16)
        for pair in range(pairs):
            lanes = pl.ds(pair * LANES, LANES)
            keys_t[pair, 0:LANES, where] = held[block, 1, :, lanes].T
            keys_t[pair, LANES : 2 * LANES, where] = feature
            values_1[pair, where, 0:LANES] = held[block, 2, :, lanes]
            values_1[pair, where, LANES : 2 * LANES] = jnp.ones((tok, LANES), jnp.bfloat16)

    prepare(mine)
    for i in range(1, groups):
        source = (mine - i + groups) % groups
        drain(held.at[source], a2a_recv.at[source])
        prepare(source)

    lane = lax.broadcasted_iota(jnp.int32, (1, LANES), 1)
    pick = [
        (lane // head_size == hh).astype(jnp.float32).astype(jnp.bfloat16)
        for hh in range(LANES // head_size)
    ]

    def attend(block, store):
        @pl.loop(0, tok // tile)
        def _(i):
            start = pl.multiple_of(i * tile, tile)
            part = pl.ds(start, tile)
            region = block_region(block, (tile, LANES), 0, start)
            place = lax.broadcasted_iota(jnp.int32, (tile, LANES), 1)
            feature = jnp.where(place == 0, region, jnp.where(place == 1, 1.0 - region, 0.0))
            feature = feature.astype(jnp.bfloat16)
            for pair in range(pairs):
                query = held[block, 0, part, pair * LANES : (pair + 1) * LANES]
                result = None
                for hh, chosen in enumerate(pick):
                    factor = scale_ref[mine * group_heads + pair * len(pick) + hh] * math.log2(math.e)
                    q = jnp.concatenate([query * chosen, feature], axis=1)
                    score = jnp.dot(q, keys_t[pair], preferred_element_type=jnp.float32)
                    best = jnp.max(score, axis=1, keepdims=True)
                    weight = jnp.exp2((score - best) * factor).astype(jnp.bfloat16)
                    both = jnp.dot(weight, values_1[pair], preferred_element_type=jnp.float32)
                    o = both[:, 0:LANES] / both[:, LANES : 2 * LANES]
                    result = o if result is None else jnp.where(place // head_size == hh, o, result)
                store(part, pair, result.astype(jnp.bfloat16))

    def give_back(step):
        block = (mine + 1 + step) % groups
        return pltpu.make_async_remote_copy(
            src_ref=heads_out.at[step],
            dst_ref=attended.at[mine],
            send_sem=back_send.at[step], recv_sem=back_recv.at[mine],
            device_id=(me, block), device_id_type=MESH,
        )

    @pl.loop(0, groups - 1)
    def _(step):
        def store(part, pair, value):
            heads_out[step, part, pair * LANES : (pair + 1) * LANES] = value

        attend((mine + 1 + step) % groups, store)
        give_back(step).start()

    def store_own(part, pair, value):
        attended[mine, part, pair * LANES : (pair + 1) * LANES] = value

    attend(mine, store_own)
    phase3(groups).wait_recv()
    for i in range(1, groups):
        source = (mine - i + groups) % groups
        drain(attended.at[source], back_recv.at[source])

    out_tile = min(width, 512)
    inner = groups * cols

    @pl.loop(0, width // out_tile)
    def _(i):
        window = pl.ds(pl.multiple_of(i * out_tile, out_tile), out_tile)
        w = w_out[:, :, :, :, window].reshape(inner, out_tile)
        x = jnp.concatenate([attended[g] for g in range(groups)], axis=1)
        y = jnp.dot(x, w, preferred_element_type=jnp.float32)
        out_ref[:, window] = (tokens_ref[:, window].astype(jnp.float32) + y).astype(jnp.bfloat16)

    for step in range(groups + 1):
        for half in range(2):
            drain(phase1_size(step, half), p1_send.at[step, half])
            drain(phase2_size(step, half), p2_send.at[step, half])
        phase3(step).wait_send()
    for step in range(groups - 1):
        exchange(step).wait_send()
        give_back(step).wait_send()


def per_device(tokens, block_map, shift, ln_gain, w_query, w_key, w_value, w_out, logit_scale):
    tok, width = tokens.shape
    heads = logit_scale.shape[0]
    inner = w_query.shape[1]
    head_size = inner // heads
    members = lax.axis_size("fsdp")
    groups = lax.axis_size("win")
    chips = members // 2
    rows_b = 2 ** ((chips.bit_length() - 1) // 2)
    rows_a = chips // rows_b
    cols = inner // groups
    rows = w_query.shape[0]
    out_rows = w_out.shape[0]
    vmem = pl.BlockSpec(memory_space=pltpu.VMEM)
    smem = pl.BlockSpec(memory_space=pltpu.SMEM)
    far = pl.BlockSpec(memory_space=pl.ANY)
    dma = pltpu.SemaphoreType.DMA
    bf16 = jnp.bfloat16
    return pl.pallas_call(
        functools.partial(layer_kernel, (rows_a, rows_b, groups, head_size)),
        out_shape=jax.ShapeDtypeStruct((tok, width), bf16),
        in_specs=[vmem, smem, smem, vmem, far, far, far, far, smem],
        out_specs=vmem,
        scratch_shapes=[
            pltpu.VMEM((groups, 3, rows_a, rows_b, 2, rows, cols), bf16),
            pltpu.VMEM((rows_a, rows_b, 2, out_rows, width), bf16),
            pltpu.VMEM((tok, width), bf16),
            pltpu.VMEM((groups - 1, 3, tok, cols), bf16),
            pltpu.VMEM((groups, 3, tok, cols), bf16),
            pltpu.VMEM((cols // LANES, 2 * LANES, groups * tok), bf16),
            pltpu.VMEM((cols // LANES, groups * tok, 2 * LANES), bf16),
            pltpu.VMEM((groups - 1, tok, cols), bf16),
            pltpu.VMEM((groups, tok, cols), bf16),
            dma((groups + 1, 3)),
            dma((groups + 1, 2)),
            dma((groups + 1, 2)),
            dma((groups + 1, 2)),
            dma((groups + 1, 2)),
            dma((groups + 1,)),
            dma((groups + 1,)),
            dma((groups,)),
            dma((groups,)),
            dma((groups,)),
            dma((groups,)),
        ],
        compiler_params=pltpu.CompilerParams(
            collective_id=0, has_side_effects=True, vmem_limit_bytes=60 * 1024 * 1024
        ),
    )(tokens, block_map, shift, ln_gain.reshape(1, width), w_query, w_key, w_value, w_out, logit_scale)


def solution(mesh):
    return jax.shard_map(
        per_device,
        mesh=mesh,
        in_specs=(
            P(("fsdp", "win"), None),
            P("fsdp", None),
            P("fsdp"),
            P(),
            P("fsdp", None),
            P("fsdp", None),
            P("fsdp", None),
            P("fsdp", None),
            P(),
        ),
        out_specs=P(("fsdp", "win"), None),
        check_vma=False,
    )
```

```python
import functools
import math

import jax
import jax.numpy as jnp
from jax import lax
from jax.experimental import pallas as pl
from jax.experimental.pallas import tpu as pltpu
from jax.sharding import PartitionSpec as P

MESH = pl.DeviceIdType.MESH
LANES = 128
FAR = 1024.0


def layer_kernel(
    sizes,
    tokens_ref, map_ref, shift_ref, gain_ref, wq_ref, wk_ref, wv_ref, wo_ref, scale_ref,
    out_ref,
    weights, w_out, normed, sent, held, keys_t, values_1, heads_out, attended,
    load_sem, p1_send, p1_recv, p2_send, p2_recv, p3_send, p3_recv,
    a2a_send, a2a_recv, back_send, back_recv,
):
    rows_a, rows_b, groups, head_size, pairs = sizes
    tok, width = tokens_ref.shape
    rows = wq_ref.shape[0]
    cols = pairs * LANES
    group_heads = cols // head_size
    last = groups * pairs
    me = lax.axis_index("fsdp")
    mine = lax.axis_index("win")
    at_a = me // (2 * rows_b)
    at_b = (me // 2) % rows_b
    at_c = me % 2

    def index_of(a, b, c):
        return (a * rows_b + b) * 2 + c

    a_peers = [index_of((at_a + i) % rows_a, at_b, at_c) for i in range(1, rows_a)]
    b_peers = [index_of(at_a, (at_b + i) % rows_b, at_c) for i in range(1, rows_b)]
    c_peer = index_of(at_a, at_b, 1 - at_c)

    barrier = pltpu.get_barrier_semaphore()
    greeted = 0
    for peer in a_peers + b_peers + [c_peer]:
        pl.semaphore_signal(barrier, inc=1, device_id=(peer, mine), device_id_type=MESH)
        greeted += 1
    for i in range(1, groups):
        pl.semaphore_signal(
            barrier, inc=1, device_id=(me, (mine + i) % groups), device_id_type=MESH
        )
        greeted += 1

    offsets = [(i + groups // 2 - 1) % groups + 1 for i in range(groups)]
    offsets = [i for i in offsets if i != groups] + [0]

    def group_of(step):
        return (mine + offsets[step % groups]) % groups

    def loads(step):
        if step == last:
            return [pltpu.make_async_copy(wo_ref, w_out.at[at_a, at_b, at_c], load_sem.at[step, 0])]
        first = group_of(step) * cols + (step // groups) * LANES
        window = pl.ds(pl.multiple_of(first, LANES), LANES)
        return [
            pltpu.make_async_copy(
                source.at[:, window],
                weights.at[step, at_a, at_b, at_c, :, pl.ds(m * LANES, LANES)],
                load_sem.at[step, m],
            )
            for m, source in enumerate((wq_ref, wk_ref, wv_ref))
        ]

    for step in range(last + 1):
        for copy in loads(step):
            copy.start()
    pl.semaphore_wait(barrier, greeted)

    def view(step, a, b, c, half):
        if step == last:
            part = w_out.shape[-1] // 2
            return w_out.at[a, b, c, :, pl.ds(half * part, part)]
        part = rows // 2
        return weights.at[step, a, b, c, pl.ds(half * part, part), :]

    def everything(count):
        return pl.ds(0, count)

    def push(ref, send, recv, peer):
        return pltpu.make_async_remote_copy(
            src_ref=ref, dst_ref=ref, send_sem=send, recv_sem=recv,
            device_id=(peer, mine), device_id_type=MESH,
        )

    def phase1(step):
        for half, peers in ((0, a_peers), (1, b_peers)):
            for peer in peers:
                push(
                    view(step, at_a, at_b, at_c, half),
                    p1_send.at[step, half], p1_recv.at[step, half], peer,
                ).start()

    def phase1_size(step, half):
        if half == 0:
            return view(step, pl.ds(0, rows_a - 1), at_b, at_c, 0)
        return view(step, at_a, pl.ds(0, rows_b - 1), at_c, 1)

    def phase2(step):
        for peer in b_peers:
            push(
                view(step, everything(rows_a), at_b, at_c, 0),
                p2_send.at[step, 0], p2_recv.at[step, 0], peer,
            ).start()
        for peer in a_peers:
            push(
                view(step, at_a, everything(rows_b), at_c, 1),
                p2_send.at[step, 1], p2_recv.at[step, 1], peer,
            ).start()

    def phase2_size(step, half):
        if half == 0:
            return view(step, everything(rows_a), pl.ds(0, rows_b - 1), at_c, 0)
        return view(step, pl.ds(0, rows_a - 1), everything(rows_b), at_c, 1)

    def phase3(step):
        ref = w_out.at[:, :, at_c] if step == last else weights.at[step, :, :, at_c]
        return push(ref, p3_send.at[step], p3_recv.at[step], c_peer)

    def drain(ref, sem):
        pltpu.make_async_copy(ref, ref, sem).wait()

    def wait1(step):
        for half in range(2):
            drain(phase1_size(step, half), p1_recv.at[step, half])

    def wait2(step):
        for half in range(2):
            drain(phase2_size(step, half), p2_recv.at[step, half])

    def own_loaded(step):
        for copy in loads(step):
            copy.wait()

    norm_tile = min(tok // 2, 64)

    def normalize(half):
        @pl.loop(0, tok // 2 // norm_tile)
        def _(i):
            start = half * (tok // 2) + i * norm_tile
            part = pl.ds(pl.multiple_of(start, norm_tile), norm_tile)
            resid = tokens_ref[part, :].astype(jnp.float32)
            center = jnp.mean(resid, axis=-1, keepdims=True)
            centred = resid - center
            spread = jnp.mean(centred * centred, axis=-1, keepdims=True)
            value = centred * lax.rsqrt(spread + 1e-05) * gain_ref[...]
            normed[part, :] = value.astype(jnp.bfloat16)

    own_loaded(0)
    phase1(0)
    normalize(0)

    tile = min(tok, 256)
    row_head = lax.broadcasted_iota(jnp.int32, (LANES, LANES), 0) // head_size
    col_head = lax.broadcasted_iota(jnp.int32, (LANES, LANES), 1) // head_size
    same_head = (row_head == col_head).astype(jnp.float32).astype(jnp.bfloat16)

    def unit(x):
        square = x * x
        high = square.astype(jnp.bfloat16)
        low = (square - high.astype(jnp.float32)).astype(jnp.bfloat16)
        total = jnp.dot(high, same_head, preferred_element_type=jnp.float32)
        total += jnp.dot(low, same_head, preferred_element_type=jnp.float32)
        return (x * lax.rsqrt(total + 1e-06)).astype(jnp.bfloat16)

    def slot(step):
        return (step // groups) * (groups - 1) + step % groups

    def exchange(step):
        pair = step // groups
        return pltpu.make_async_remote_copy(
            src_ref=sent.at[slot(step)], dst_ref=held.at[pair, mine],
            send_sem=a2a_send.at[slot(step)], recv_sem=a2a_recv.at[pair, mine],
            device_id=(me, group_of(step)), device_id_type=MESH,
        )

    remote_steps = [step for step in range(last) if step % groups < groups - 1]

    def project(step):
        remote = step in remote_steps
        target = sent.at[slot(step)] if remote else held.at[step // groups, mine]

        @pl.loop(0, tok // tile)
        def _(i):
            part = pl.ds(pl.multiple_of(i * tile, tile), tile)
            w = weights[step].reshape(width, 3 * LANES)
            y = jnp.dot(normed[part, :], w, preferred_element_type=jnp.float32)
            target[0, part, :] = unit(y[:, 0:LANES])
            target[1, part, :] = unit(y[:, LANES : 2 * LANES])
            target[2, part, :] = y[:, 2 * LANES :].astype(jnp.bfloat16)

        if remote:
            exchange(step).start()

    for step in range(last + 1):
        wait1(step)
        phase2(step)
        if step < last:
            own_loaded(step + 1)
            phase1(step + 1)
        if step == 0:
            normalize(1)
        else:
            wait2(step - 1)
            phase3(step - 1).start()
            phase3(step - 1).wait_recv()
            project(step - 1)

    def block_region(block, shape, axis, start):
        first = map_ref[0, block] * tok + start
        return (first + lax.broadcasted_iota(jnp.int32, shape, axis) >= shift_ref[0]).astype(jnp.float32)

    def prepare(pair, block):
        where = pl.ds(pl.multiple_of(block * tok, tok), tok)
        region = block_region(block, (LANES, tok), 1, 0)
        row = lax.broadcasted_iota(jnp.int32, (LANES, tok), 0)
        feature = jnp.where(row == 0, region - 1.0, jnp.where(row == 1, -region, 0.0)) * FAR
        keys_t[pair, 0:LANES, where] = held[pair, block, 1].T
        keys_t[pair, LANES : 2 * LANES, where] = feature.astype(jnp.bfloat16)
        values_1[pair, where, 0:LANES] = held[pair, block, 2]
        values_1[pair, where, LANES : 2 * LANES] = jnp.ones((tok, LANES), jnp.bfloat16)

    def prepare_all(pair):
        prepare(pair, mine)
        for offset in offsets[:-1]:
            source = (mine - offset + groups) % groups
            drain(held.at[pair, source], a2a_recv.at[pair, source])
            prepare(pair, source)

    lane = lax.broadcasted_iota(jnp.int32, (1, LANES), 1)
    pick = [
        (lane // head_size == hh).astype(jnp.float32).astype(jnp.bfloat16)
        for hh in range(LANES // head_size)
    ]

    def attend(pair, block, target):
        @pl.loop(0, tok // tile)
        def _(i):
            start = pl.multiple_of(i * tile, tile)
            part = pl.ds(start, tile)
            region = block_region(block, (tile, LANES), 0, start)
            place = lax.broadcasted_iota(jnp.int32, (tile, LANES), 1)
            feature = jnp.where(place == 0, region, jnp.where(place == 1, 1.0 - region, 0.0))
            feature = feature.astype(jnp.bfloat16)
            query = held[pair, block, 0, part, :]
            result = None
            for hh, chosen in enumerate(pick):
                factor = scale_ref[mine * group_heads + pair * len(pick) + hh] * math.log2(math.e)
                q = jnp.concatenate([query * chosen, feature], axis=1)
                score = jnp.dot(q, keys_t[pair], preferred_element_type=jnp.float32)
                best = jnp.max(score, axis=1, keepdims=True)
                weight = jnp.exp2((score - best) * factor).astype(jnp.bfloat16)
                both = jnp.dot(weight, values_1[pair], preferred_element_type=jnp.float32)
                o = both[:, 0:LANES] / both[:, LANES : 2 * LANES]
                result = o if result is None else jnp.where(place // head_size == hh, o, result)
            target[part, :] = result.astype(jnp.bfloat16)

    def give_back(step):
        pair = step // groups
        return pltpu.make_async_remote_copy(
            src_ref=heads_out.at[slot(step)], dst_ref=attended.at[mine, pair],
            send_sem=back_send.at[slot(step)], recv_sem=back_recv.at[pair, mine],
            device_id=(me, group_of(step)), device_id_type=MESH,
        )

    for step in range(last):
        pair = step // groups
        if step % groups == 0:
            prepare_all(pair)
        if step in remote_steps:
            attend(pair, group_of(step), heads_out.at[slot(step)])
            give_back(step).start()
        else:
            attend(pair, mine, attended.at[mine, pair])
        if step == 0:
            wait2(last)
            phase3(last).start()

    phase3(last).wait_recv()
    for pair in range(pairs):
        for offset in offsets[:-1]:
            source = (mine - offset + groups) % groups
            drain(attended.at[source, pair], back_recv.at[pair, source])

    out_tile = min(width, 512)
    inner = groups * cols

    @pl.loop(0, width // out_tile)
    def _(i):
        window = pl.ds(pl.multiple_of(i * out_tile, out_tile), out_tile)
        w = w_out[:, :, :, :, window].reshape(inner, out_tile)
        x = jnp.concatenate(
            [attended[g, pair] for g in range(groups) for pair in range(pairs)], axis=1
        )
        y = jnp.dot(x, w, preferred_element_type=jnp.float32)
        out_ref[:, window] = (tokens_ref[:, window].astype(jnp.float32) + y).astype(jnp.bfloat16)

    for step in range(last + 1):
        for half in range(2):
            drain(phase1_size(step, half), p1_send.at[step, half])
            drain(phase2_size(step, half), p2_send.at[step, half])
        phase3(step).wait_send()
    for step in remote_steps:
        exchange(step).wait_send()
        give_back(step).wait_send()


def per_device(tokens, block_map, shift, ln_gain, w_query, w_key, w_value, w_out, logit_scale):
    tok, width = tokens.shape
    heads = logit_scale.shape[0]
    inner = w_query.shape[1]
    head_size = inner // heads
    members = lax.axis_size("fsdp")
    groups = lax.axis_size("win")
    chips = members // 2
    rows_b = 2 ** ((chips.bit_length() - 1) // 2)
    rows_a = chips // rows_b
    pairs = inner // groups // LANES
    steps = groups * pairs
    rows = w_query.shape[0]
    out_rows = w_out.shape[0]
    vmem = pl.BlockSpec(memory_space=pltpu.VMEM)
    smem = pl.BlockSpec(memory_space=pltpu.SMEM)
    far = pl.BlockSpec(memory_space=pl.ANY)
    dma = pltpu.SemaphoreType.DMA
    bf16 = jnp.bfloat16
    return pl.pallas_call(
        functools.partial(layer_kernel, (rows_a, rows_b, groups, head_size, pairs)),
        out_shape=jax.ShapeDtypeStruct((tok, width), bf16),
        in_specs=[vmem, smem, smem, vmem, far, far, far, far, smem],
        out_specs=vmem,
        scratch_shapes=[
            pltpu.VMEM((steps, rows_a, rows_b, 2, rows, 3 * LANES), bf16),
            pltpu.VMEM((rows_a, rows_b, 2, out_rows, width), bf16),
            pltpu.VMEM((tok, width), bf16),
            pltpu.VMEM((pairs * (groups - 1), 3, tok, LANES), bf16),
            pltpu.VMEM((pairs, groups, 3, tok, LANES), bf16),
            pltpu.VMEM((pairs, 2 * LANES, groups * tok), bf16),
            pltpu.VMEM((pairs, groups * tok, 2 * LANES), bf16),
            pltpu.VMEM((pairs * (groups - 1), tok, LANES), bf16),
            pltpu.VMEM((groups, pairs, tok, LANES), bf16),
            dma((steps + 1, 3)),
            dma((steps + 1, 2)),
            dma((steps + 1, 2)),
            dma((steps + 1, 2)),
            dma((steps + 1, 2)),
            dma((steps + 1,)),
            dma((steps + 1,)),
            dma((pairs * (groups - 1),)),
            dma((pairs, groups)),
            dma((pairs * (groups - 1),)),
            dma((pairs, groups)),
        ],
        compiler_params=pltpu.CompilerParams(
            collective_id=0, has_side_effects=True, vmem_limit_bytes=60 * 1024 * 1024
        ),
    )(tokens, block_map, shift, ln_gain.reshape(1, width), w_query, w_key, w_value, w_out, logit_scale)


def solution(mesh):
    return jax.shard_map(
        per_device,
        mesh=mesh,
        in_specs=(
            P(("fsdp", "win"), None),
            P("fsdp", None),
            P("fsdp"),
            P(),
            P("fsdp", None),
            P("fsdp", None),
            P("fsdp", None),
            P("fsdp", None),
            P(),
        ),
        out_specs=P(("fsdp", "win"), None),
        check_vma=False,
    )
```

```python
import functools
import math

import jax
import jax.numpy as jnp
from jax import lax
from jax.experimental import pallas as pl
from jax.experimental.pallas import tpu as pltpu
from jax.sharding import PartitionSpec as P

MESH = pl.DeviceIdType.MESH
LANES = 128
FAR = 1024.0


def layer_kernel(
    sizes,
    tokens_ref, map_ref, shift_ref, gain_ref, wq_ref, wk_ref, wv_ref, wo_ref, scale_ref,
    out_ref,
    weights, w_out, normed, sent, held, keys_t, values_1, heads_out, attended,
    load_sem, p1_send, p1_recv, p2_send, p2_recv, p3_send, p3_recv,
    a2a_send, a2a_recv, back_send, back_recv,
):
    rows_a, rows_b, groups, head_size, pairs = sizes
    tok, width = tokens_ref.shape
    rows = wq_ref.shape[0]
    cols = pairs * LANES
    group_heads = cols // head_size
    last = groups * pairs
    me = lax.axis_index("fsdp")
    mine = lax.axis_index("win")
    at_a = me // (2 * rows_b)
    at_b = (me // 2) % rows_b
    at_c = me % 2

    def index_of(a, b, c):
        return (a * rows_b + b) * 2 + c

    a_peers = [index_of((at_a + i) % rows_a, at_b, at_c) for i in range(1, rows_a)]
    b_peers = [index_of(at_a, (at_b + i) % rows_b, at_c) for i in range(1, rows_b)]
    c_peer = index_of(at_a, at_b, 1 - at_c)

    barrier = pltpu.get_barrier_semaphore()
    greeted = 0
    for peer in a_peers + b_peers + [c_peer]:
        pl.semaphore_signal(barrier, inc=1, device_id=(peer, mine), device_id_type=MESH)
        greeted += 1
    for i in range(1, groups):
        pl.semaphore_signal(
            barrier, inc=1, device_id=(me, (mine + i) % groups), device_id_type=MESH
        )
        greeted += 1

    offsets = [(i + groups // 2 - 1) % groups + 1 for i in range(groups)]
    offsets = [i for i in offsets if i != groups] + [0]

    def group_of(step):
        return (mine + offsets[step % groups]) % groups

    def loads(step):
        if step == last:
            return [pltpu.make_async_copy(wo_ref, w_out.at[at_a, at_b, at_c], load_sem.at[step, 0])]
        first = group_of(step) * cols + (step // groups) * LANES
        window = pl.ds(pl.multiple_of(first, LANES), LANES)
        return [
            pltpu.make_async_copy(
                source.at[:, window],
                weights.at[step, at_a, at_b, at_c, :, pl.ds(m * LANES, LANES)],
                load_sem.at[step, m],
            )
            for m, source in enumerate((wq_ref, wk_ref, wv_ref))
        ]

    for step in range(last + 1):
        for copy in loads(step):
            copy.start()
    pl.semaphore_wait(barrier, greeted)

    def view(step, a, b, c, half):
        if step == last:
            part = w_out.shape[-1] // 2
            return w_out.at[a, b, c, :, pl.ds(half * part, part)]
        part = rows // 2
        return weights.at[step, a, b, c, pl.ds(half * part, part), :]

    def everything(count):
        return pl.ds(0, count)

    def push(ref, send, recv, peer):
        return pltpu.make_async_remote_copy(
            src_ref=ref, dst_ref=ref, send_sem=send, recv_sem=recv,
            device_id=(peer, mine), device_id_type=MESH,
        )

    def phase1(step):
        for half, peers in ((0, a_peers), (1, b_peers)):
            for peer in peers:
                push(
                    view(step, at_a, at_b, at_c, half),
                    p1_send.at[step, half], p1_recv.at[step, half], peer,
                ).start()

    def phase1_size(step, half):
        if half == 0:
            return view(step, pl.ds(0, rows_a - 1), at_b, at_c, 0)
        return view(step, at_a, pl.ds(0, rows_b - 1), at_c, 1)

    def phase2(step):
        for peer in b_peers:
            push(
                view(step, everything(rows_a), at_b, at_c, 0),
                p2_send.at[step, 0], p2_recv.at[step, 0], peer,
            ).start()
        for peer in a_peers:
            push(
                view(step, at_a, everything(rows_b), at_c, 1),
                p2_send.at[step, 1], p2_recv.at[step, 1], peer,
            ).start()

    def phase2_size(step, half):
        if half == 0:
            return view(step, everything(rows_a), pl.ds(0, rows_b - 1), at_c, 0)
        return view(step, pl.ds(0, rows_a - 1), everything(rows_b), at_c, 1)

    def phase3(step):
        ref = w_out.at[:, :, at_c] if step == last else weights.at[step, :, :, at_c]
        return push(ref, p3_send.at[step], p3_recv.at[step], c_peer)

    def drain(ref, sem):
        pltpu.make_async_copy(ref, ref, sem).wait()

    def wait1(step):
        for half in range(2):
            drain(phase1_size(step, half), p1_recv.at[step, half])

    def wait2(step):
        for half in range(2):
            drain(phase2_size(step, half), p2_recv.at[step, half])

    def own_loaded(step):
        for copy in loads(step):
            copy.wait()

    norm_tile = min(tok // 2, 64)

    def normalize(half):
        @pl.loop(0, tok // 2 // norm_tile)
        def _(i):
            start = half * (tok // 2) + i * norm_tile
            part = pl.ds(pl.multiple_of(start, norm_tile), norm_tile)
            resid = tokens_ref[part, :].astype(jnp.float32)
            center = jnp.mean(resid, axis=-1, keepdims=True)
            centred = resid - center
            spread = jnp.mean(centred * centred, axis=-1, keepdims=True)
            value = centred * lax.rsqrt(spread + 1e-05) * gain_ref[...]
            normed[part, :] = value.astype(jnp.bfloat16)

    own_loaded(0)
    phase1(0)
    normalize(0)

    tile = min(tok, 256)
    row_head = lax.broadcasted_iota(jnp.int32, (LANES, LANES), 0) // head_size
    col_head = lax.broadcasted_iota(jnp.int32, (LANES, LANES), 1) // head_size
    same_head = (row_head == col_head).astype(jnp.float32).astype(jnp.bfloat16)

    def unit(x):
        square = x * x
        high = square.astype(jnp.bfloat16)
        low = (square - high.astype(jnp.float32)).astype(jnp.bfloat16)
        total = jnp.dot(high, same_head, preferred_element_type=jnp.float32)
        total += jnp.dot(low, same_head, preferred_element_type=jnp.float32)
        return (x * lax.rsqrt(total + 1e-06)).astype(jnp.bfloat16)

    def slot(step):
        return (step // groups) * (groups - 1) + step % groups

    def exchange(step):
        pair = step // groups
        return pltpu.make_async_remote_copy(
            src_ref=sent.at[slot(step)], dst_ref=held.at[pair, mine],
            send_sem=a2a_send.at[slot(step)], recv_sem=a2a_recv.at[pair, mine],
            device_id=(me, group_of(step)), device_id_type=MESH,
        )

    remote_steps = [step for step in range(last) if step % groups < groups - 1]

    def project(step):
        remote = step in remote_steps
        target = sent.at[slot(step)] if remote else held.at[step // groups, mine]

        @pl.loop(0, tok // tile)
        def _(i):
            part = pl.ds(pl.multiple_of(i * tile, tile), tile)
            w = weights[step].reshape(width, 3 * LANES)
            y = jnp.dot(normed[part, :], w, preferred_element_type=jnp.float32)
            target[0, part, :] = unit(y[:, 0:LANES])
            target[1, part, :] = unit(y[:, LANES : 2 * LANES])
            target[2, part, :] = y[:, 2 * LANES :].astype(jnp.bfloat16)

        if remote:
            exchange(step).start()

    order = remote_steps + [step for step in range(last) if step not in remote_steps] + [last]
    for turn, step in enumerate(order):
        wait1(step)
        phase2(step)
        if turn == 0:
            normalize(1)
        if step != last:
            own_loaded(order[turn + 1])
            phase1(order[turn + 1])
        if turn > 0:
            before = order[turn - 1]
            wait2(before)
            phase3(before).start()
            phase3(before).wait_recv()
            project(before)

    def block_region(block, shape, axis, start):
        first = map_ref[0, block] * tok + start
        return (first + lax.broadcasted_iota(jnp.int32, shape, axis) >= shift_ref[0]).astype(jnp.float32)

    def prepare(pair, block):
        where = pl.ds(pl.multiple_of(block * tok, tok), tok)
        region = block_region(block, (LANES, tok), 1, 0)
        row = lax.broadcasted_iota(jnp.int32, (LANES, tok), 0)
        feature = jnp.where(row == 0, region - 1.0, jnp.where(row == 1, -region, 0.0)) * FAR
        keys_t[pair, 0:LANES, where] = held[pair, block, 1].T
        keys_t[pair, LANES : 2 * LANES, where] = feature.astype(jnp.bfloat16)
        values_1[pair, where, 0:LANES] = held[pair, block, 2]
        values_1[pair, where, LANES : 2 * LANES] = jnp.ones((tok, LANES), jnp.bfloat16)

    def prepare_all(pair):
        prepare(pair, mine)
        for offset in offsets[:-1]:
            source = (mine - offset + groups) % groups
            drain(held.at[pair, source], a2a_recv.at[pair, source])
            if pair > 0 and offset == offsets[-2]:
                for step in remote_steps:
                    if step // groups == pair - 1:
                        give_back(step).start()
            prepare(pair, source)

    lane = lax.broadcasted_iota(jnp.int32, (1, LANES), 1)
    pick = [
        (lane // head_size == hh).astype(jnp.float32).astype(jnp.bfloat16)
        for hh in range(LANES // head_size)
    ]

    def attend(pair, block, target):
        @pl.loop(0, tok // tile)
        def _(i):
            start = pl.multiple_of(i * tile, tile)
            part = pl.ds(start, tile)
            region = block_region(block, (tile, LANES), 0, start)
            place = lax.broadcasted_iota(jnp.int32, (tile, LANES), 1)
            feature = jnp.where(place == 0, region, jnp.where(place == 1, 1.0 - region, 0.0))
            feature = feature.astype(jnp.bfloat16)
            query = held[pair, block, 0, part, :]
            result = None
            for hh, chosen in enumerate(pick):
                factor = scale_ref[mine * group_heads + pair * len(pick) + hh] * math.log2(math.e)
                q = jnp.concatenate([query * chosen, feature], axis=1)
                score = jnp.dot(q, keys_t[pair], preferred_element_type=jnp.float32)
                best = jnp.max(score, axis=1, keepdims=True)
                weight = jnp.exp2((score - best) * factor).astype(jnp.bfloat16)
                both = jnp.dot(weight, values_1[pair], preferred_element_type=jnp.float32)
                o = both[:, 0:LANES] / both[:, LANES : 2 * LANES]
                result = o if result is None else jnp.where(place // head_size == hh, o, result)
            target[part, :] = result.astype(jnp.bfloat16)

    def give_back(step):
        pair = step // groups
        return pltpu.make_async_remote_copy(
            src_ref=heads_out.at[slot(step)], dst_ref=attended.at[mine, pair],
            send_sem=back_send.at[slot(step)], recv_sem=back_recv.at[pair, mine],
            device_id=(me, group_of(step)), device_id_type=MESH,
        )

    for step in range(last):
        pair = step // groups
        if step % groups == 0:
            prepare_all(pair)
        if step in remote_steps:
            attend(pair, group_of(step), heads_out.at[slot(step)])
            if pair == pairs - 1:
                give_back(step).start()
        else:
            attend(pair, mine, attended.at[mine, pair])
        if step == 0:
            wait2(last)
            phase3(last).start()

    phase3(last).wait_recv()
    for pair in range(pairs):
        for offset in offsets[:-1]:
            source = (mine - offset + groups) % groups
            drain(attended.at[source, pair], back_recv.at[pair, source])

    out_tile = min(width, 512)
    inner = groups * cols

    @pl.loop(0, width // out_tile)
    def _(i):
        window = pl.ds(pl.multiple_of(i * out_tile, out_tile), out_tile)
        w = w_out[:, :, :, :, window].reshape(inner, out_tile)
        x = jnp.concatenate(
            [attended[g, pair] for g in range(groups) for pair in range(pairs)], axis=1
        )
        y = jnp.dot(x, w, preferred_element_type=jnp.float32)
        out_ref[:, window] = (tokens_ref[:, window].astype(jnp.float32) + y).astype(jnp.bfloat16)

    for step in range(last + 1):
        for half in range(2):
            drain(phase1_size(step, half), p1_send.at[step, half])
            drain(phase2_size(step, half), p2_send.at[step, half])
        phase3(step).wait_send()
    for step in remote_steps:
        exchange(step).wait_send()
        give_back(step).wait_send()


def per_device(tokens, block_map, shift, ln_gain, w_query, w_key, w_value, w_out, logit_scale):
    tok, width = tokens.shape
    heads = logit_scale.shape[0]
    inner = w_query.shape[1]
    head_size = inner // heads
    members = lax.axis_size("fsdp")
    groups = lax.axis_size("win")
    chips = members // 2
    rows_b = 2 ** ((chips.bit_length() - 1) // 2)
    rows_a = chips // rows_b
    pairs = inner // groups // LANES
    steps = groups * pairs
    rows = w_query.shape[0]
    out_rows = w_out.shape[0]
    vmem = pl.BlockSpec(memory_space=pltpu.VMEM)
    smem = pl.BlockSpec(memory_space=pltpu.SMEM)
    far = pl.BlockSpec(memory_space=pl.ANY)
    dma = pltpu.SemaphoreType.DMA
    bf16 = jnp.bfloat16
    return pl.pallas_call(
        functools.partial(layer_kernel, (rows_a, rows_b, groups, head_size, pairs)),
        out_shape=jax.ShapeDtypeStruct((tok, width), bf16),
        in_specs=[vmem, smem, smem, vmem, far, far, far, far, smem],
        out_specs=vmem,
        scratch_shapes=[
            pltpu.VMEM((steps, rows_a, rows_b, 2, rows, 3 * LANES), bf16),
            pltpu.VMEM((rows_a, rows_b, 2, out_rows, width), bf16),
            pltpu.VMEM((tok, width), bf16),
            pltpu.VMEM((pairs * (groups - 1), 3, tok, LANES), bf16),
            pltpu.VMEM((pairs, groups, 3, tok, LANES), bf16),
            pltpu.VMEM((pairs, 2 * LANES, groups * tok), bf16),
            pltpu.VMEM((pairs, groups * tok, 2 * LANES), bf16),
            pltpu.VMEM((pairs * (groups - 1), tok, LANES), bf16),
            pltpu.VMEM((groups, pairs, tok, LANES), bf16),
            dma((steps + 1, 3)),
            dma((steps + 1, 2)),
            dma((steps + 1, 2)),
            dma((steps + 1, 2)),
            dma((steps + 1, 2)),
            dma((steps + 1,)),
            dma((steps + 1,)),
            dma((pairs * (groups - 1),)),
            dma((pairs, groups)),
            dma((pairs * (groups - 1),)),
            dma((pairs, groups)),
        ],
        compiler_params=pltpu.CompilerParams(
            collective_id=0, has_side_effects=True, vmem_limit_bytes=60 * 1024 * 1024
        ),
    )(tokens, block_map, shift, ln_gain.reshape(1, width), w_query, w_key, w_value, w_out, logit_scale)


def solution(mesh):
    return jax.shard_map(
        per_device,
        mesh=mesh,
        in_specs=(
            P(("fsdp", "win"), None),
            P("fsdp", None),
            P("fsdp"),
            P(),
            P("fsdp", None),
            P("fsdp", None),
            P("fsdp", None),
            P("fsdp", None),
            P(),
        ),
        out_specs=P(("fsdp", "win"), None),
        check_vma=False,
    )
```
